128 devices in a mesh: lag: 8 (over y, x_lo), row: 16 (over x_hi, z, core).
Axes of the slice: x: 4 (x_hi: 2, x_lo: 2; x = x_hi * 2 + x_lo), y: 4, z: 4, core: 2. Of those that a mesh axis runs over, the one named last changes fastest.
Arguments:
- lag_weights: float32 [32, 4096, 4096], P('lag', 'row'), may hold values from -0.015625 to 0.015625
- inverse_head: float32 [4096, 4096], P('row'), may hold values from -0.09375 to 0.09375
- excitation: float32 [3, 4096, 128], P(None, 'row'), may hold values from -6 to 6
- history: float32 [32, 4096, 128], P('lag', 'row'), may hold values from -6 to 6
Outputs:
- densities: float32 [3, 4096, 128], P(None, 'row')
The draws below stay inside these ranges and needn't reach their ends.
All inputs are finite; a program needn't handle non-finite values.
Results may differ from the reference program's by a relative error of at most 0.0001.
Values sent between devices are 32-bit elements; how exact they have to be, the bound alone decides.
A program may use at most 128 MiB of HBM per device.

```python
import jax
import jax.numpy as jnp
from jax import lax

M = 4096
EXC = 128
STEPS = 3
LAGS = 32


def block_levels(stream_key, extent, cuts, smallest, largest):
    level = 1.0
    for axis_at, shards_of in cuts:
        draws = jax.random.uniform(jax.random.fold_in(jax.random.fold_in(stream_key, 6), axis_at), (shards_of,), jnp.float32, smallest / len(cuts), largest / len(cuts))
        level = level * jnp.repeat(jnp.exp(draws), extent[axis_at] // shards_of).reshape((-1,) + (1,) * (len(extent) - 1 - axis_at))
    return level


def centred(stream_key, dims, deviation, bound, shards=(), kind=jnp.bfloat16):
    result = jax.random.normal(stream_key, dims, jnp.float32) * deviation
    if len(shards) > 0:
        result = block_levels(stream_key, dims, shards, -0.22, 0.18) * result
    return jnp.clip(result, min=-bound, max=bound).astype(kind)


def setup_inputs(seed: int = 0) -> dict:
    arg_keys = jax.random.split(jax.random.key(seed), 5)
    lag_weights = centred(arg_keys[0], (LAGS, M, M), (M * LAGS) ** -0.5, 0.015625, ((0, 8), (1, 16)), jnp.float32)
    inverse_head = centred(arg_keys[1], (M, M), M ** -0.5, 0.09375, ((0, 16),), jnp.float32)
    excitation = centred(arg_keys[2], (STEPS, M, EXC), 1.0, 6.0, ((1, 16),), jnp.float32)
    history = centred(arg_keys[3], (LAGS, M, EXC), 1.0, 6.0, ((0, 8), (1, 16)), jnp.float32)
    return {"lag_weights": lag_weights, "inverse_head": inverse_head, "excitation": excitation, "history": history}


def reference(lag_weights, inverse_head, excitation, history):
    past = history
    results = []
    for step in range(STEPS):
        carried = jnp.einsum("kmc,kcr->mr", lag_weights, past, precision=lax.Precision.HIGHEST)
        density = jnp.dot(inverse_head, excitation[step] - carried, precision=lax.Precision.HIGHEST, preferred_element_type=jnp.float32)
        results.append(density)
        past = jnp.concatenate([density[None], past[:-1]], axis=0)
    return jnp.stack(results, axis=0)
```

```python
import jax
import jax.numpy as jnp
from jax import lax
from jax.experimental import pallas as pl
from jax.experimental.pallas import tpu as pltpu
from jax.sharding import PartitionSpec as P

STEPS = 3
LAGS = 4
ROWS = 256
M = 4096
EXC = 128
BLOCK = 512
F32 = jnp.float32
BF16 = jnp.bfloat16
MESH = pl.DeviceIdType.MESH
NT = (((1,), (1,)), ((), ()))
NEAR = ((0, 0), (0, 1), (0, 3), (1, 0), (0, 2), (1, 1), (1, 3), (1, 2))


def halves(value):
    high = value.astype(BF16)
    return high, (value - high.astype(F32)).astype(BF16)


def kernel(
    w_hbm, h_hbm, x_hbm, p_hbm, out_ref,
    wv, pg, h_own, h_sib, ht_hi, ht_lo, w12, xv, acc,
    ct, hb, ub, rb, ab, db, mb, ob, sb,
    local_sem, p_send, p_recv, s_send, s_recv, e_send, e_recv, es_send, es_recv,
    w_send, w_recv, in_send, in_recv, c_send, c_recv, r_send, r_recv,
    a_send, a_recv, m_send, m_recv, o_send, o_recv, os_send, os_recv,
):
    lag = lax.axis_index("lag")
    row = lax.axis_index("row")
    chip, core = row // 2, row % 2
    y, x_lo = lag // 2, lag % 2
    x_hi, z = chip // 4, chip % 4

    def near(dx, dz):
        return ((x_hi + dx) % 2) * 4 + (z + dz) % 4

    def at_chip(other):
        return (lag, other * 2 + core)

    def lag_near(k):
        return ((y + k // 2) % 4) * 2 + (x_lo + k % 2) % 2

    def at_lag(other):
        return (other, row)

    sibling = (lag, chip * 2 + 1 - core)

    def rows_of(a_chip, a_core):
        return pl.ds(pl.multiple_of((a_chip * 2 + a_core) * ROWS, ROWS), ROWS)

    def chip_rows(a_chip):
        return pl.ds(pl.multiple_of(a_chip * BLOCK, BLOCK), BLOCK)

    def remote(src, dst, send, recv, device):
        return pltpu.make_async_remote_copy(
            src_ref=src, dst_ref=dst, send_sem=send, recv_sem=recv,
            device_id=device, device_id_type=MESH,
        )

    sends = []

    def go(copy):
        copy.start()
        sends.append(copy)

    mine = rows_of(chip, core)
    locals_ = [
        pltpu.make_async_copy(h_hbm, h_own, local_sem.at[0]),
        pltpu.make_async_copy(p_hbm, pg.at[pl.ds(2, LAGS), mine], local_sem.at[1]),
        pltpu.make_async_copy(x_hbm, xv, local_sem.at[2]),
        pltpu.make_async_copy(w_hbm, wv, local_sem.at[3]),
    ]
    for copy in locals_:
        copy.start()

    barrier = pltpu.get_barrier_semaphore()

    def greet(device):
        pl.semaphore_signal(barrier, inc=1, device_id=device, device_id_type=MESH)

    greet(sibling)
    for k in range(1, 8):
        greet(at_chip(near(k // 4, k % 4)))
        greet(at_lag(lag_near(k)))
    for other in range(8):

        @pl.when(jnp.logical_or(lag != chip, other != lag))
        def _():
            greet((other, lag * 2 + core))

    @pl.when(lag == chip)
    def _():
        pl.semaphore_wait(barrier, 22)

    @pl.when(lag != chip)
    def _():
        pl.semaphore_wait(barrier, 23)

    up, down, across = at_chip(near(0, 1)), at_chip(near(0, 3)), at_chip(near(1, 0))

    class Gather:
        def __init__(self, first, count, send, recv, ssend, srecv):
            self.first, self.count = first, count
            self.send, self.recv, self.ssend, self.srecv = send, recv, ssend, srecv
            half = count // 2
            self.all = (first, count, 0, ROWS)
            self.low = (first, half, 0, ROWS)
            self.high = (first + half, half, 0, ROWS)
            if half == 2:
                self.b1, self.b2 = (first + 2, 1, 0, ROWS), (first + 3, 1, 0, ROWS)
            else:
                self.b1, self.b2 = (first + 1, 1, 0, ROWS // 2), (first + 1, 1, ROWS // 2, ROWS // 2)

        def view(self, dx, dz, part, a_core=None):
            start, count, offset, size = part
            base = (near(dx, dz) * 2 + (core if a_core is None else a_core)) * ROWS + offset
            return pg.at[pl.ds(start, count), pl.ds(pl.multiple_of(base, ROWS // 2), size)]

        def copy(self, index, dx, dz, part, device, src=None):
            view = self.view(dx, dz, part)
            return remote(view if src is None else src, view, self.send.at[index], self.recv.at[index], device)

        def arrived(self, index, dx, dz, part):
            view = self.view(dx, dz, part)
            remote(view, view, self.send.at[index], self.recv.at[index], up).wait_recv()

        def to_sibling(self, index, dx, dz, src=None):
            view = self.view(dx, dz, self.all)
            return remote(view if src is None else src, view, self.ssend.at[index], self.srecv.at[index], sibling)

        def from_sibling(self, index, dx, dz):
            view = self.view(dx, dz, self.all, 1 - core)
            remote(view, view, self.ssend.at[index], self.srecv.at[index], sibling).wait_recv()

        def start(self, src=None):
            return [
                self.copy(0, 0, 0, self.all, up, src),
                self.copy(1, 0, 0, self.all, down, src),
                self.copy(2, 0, 0, self.all, across, src),
                self.to_sibling(0, 0, 0, src),
            ]

        def stage1(self):
            self.arrived(0, 0, 3, self.all)
            out = [self.copy(3, 0, 3, self.low, up), self.copy(5, 0, 3, self.low, across), self.to_sibling(1, 0, 3)]
            yield out
            self.arrived(1, 0, 1, self.all)
            out = [self.copy(4, 0, 1, self.high, down), self.copy(6, 0, 1, self.low, across), self.to_sibling(2, 0, 1)]
            yield out
            self.arrived(2, 1, 0, self.all)
            yield [self.copy(8, 1, 0, self.high, up), self.copy(9, 1, 0, self.high, down), self.to_sibling(3, 1, 0)]

        def stage2(self):
            self.arrived(3, 0, 2, self.low)
            yield [self.copy(7, 0, 2, self.low, across)]
            self.arrived(4, 0, 2, self.high)
            yield [self.to_sibling(4, 0, 2)]
            self.arrived(8, 1, 3, self.high)
            yield [self.copy(10, 1, 3, self.b1, up)]
            self.arrived(9, 1, 1, self.high)
            yield [self.copy(11, 1, 1, self.b2, down)]
            self.arrived(5, 1, 3, self.low)
            yield [self.to_sibling(5, 1, 3)]
            self.arrived(6, 1, 1, self.low)
            yield [self.to_sibling(6, 1, 1)]

        def stage3(self):
            self.arrived(7, 1, 2, self.low)
            self.arrived(10, 1, 2, self.b1)
            self.arrived(11, 1, 2, self.b2)
            yield [self.to_sibling(7, 1, 2)]

        def everything(self):
            return (
                [self.copy(i, 0, 0, self.all, up) for i in range(3)]
                + [self.copy(i, 0, 0, self.low, up) for i in range(3, 10)]
                + [self.copy(i, 0, 0, self.b1, up) for i in (10, 11)]
                + [self.to_sibling(i, 0, 0) for i in range(8)]
            )

    SIB = ((0, 0), (0, 3), (0, 1), (1, 0), (0, 2), (1, 3), (1, 1), (1, 2))
    past = Gather(2, LAGS, p_send, p_recv, s_send, s_recv)
    older = Gather(0, 2, e_send, e_recv, es_send, es_recv)

    for copy in past.start(p_hbm):
        copy.start()
    to_h = remote(h_hbm, h_sib, in_send.at[0], in_recv.at[0], sibling)
    to_h.start()

    e_view = pg.at[pl.ds(0, 2), mine]
    next_group = ((lag + 1) % 8, row)
    handed = remote(p_hbm.at[pl.ds(2, 2)], e_view, in_send.at[1], in_recv.at[1], next_group)

    @pl.when(lag < 7)
    def _():
        handed.start()

    def w_part(n, half):
        return w12.at[n, pl.ds(pl.multiple_of(half * ROWS, ROWS), ROWS)]

    def w_copy(n, k):
        return remote(
            w_hbm.at[n, :, pl.ds(k * BLOCK, BLOCK)], w_part(n, core), w_send.at[n], w_recv.at[n], (k, row)
        )

    def w_keep(n):
        return pltpu.make_async_copy(w_hbm.at[n, :, pl.ds(0, BLOCK)], w_part(n, core), local_sem.at[4 + n])

    @pl.when(lag == 0)
    def _():
        for n in range(2):
            w_keep(n).start()
            for k in range(1, 8):
                w_copy(n, k).start()
        pg[0:2] = jnp.zeros((2, M, EXC), F32)

    def w_sib(n):
        return remote(w_part(n, core), w_part(n, core), w_send.at[2 + n], w_recv.at[2 + n], sibling)

    def w_sib_arrived(n):
        part = w_part(n, 1 - core)
        remote(part, part, w_send.at[2 + n], w_recv.at[2 + n], sibling).wait_recv()

    def w_pass(n):
        @pl.when(lag == 0)
        def _():
            w_keep(n).wait()

        @pl.when(lag != 0)
        def _():
            remote(w_part(n, core), w_part(n, core), w_send.at[n], w_recv.at[n], sibling).wait_recv()

        w_sib(n).start()

    def block_product(n, a_chip):
        rows = chip_rows(a_chip)
        values, highs, lows = [], [], []
        for i in range(LAGS):
            values.append(jnp.concatenate(halves(pg[2 + i - n, rows, :]), axis=1))
            high, low = halves(wv[i, :, rows])
            highs.append(high)
            lows.append(low)
        value = jnp.concatenate(values, axis=0)
        acc[n] += jnp.dot(jnp.concatenate(highs, axis=1), value, preferred_element_type=F32) + jnp.dot(
            jnp.concatenate(lows, axis=1), value, preferred_element_type=F32
        )

    acc[...] = jnp.zeros(acc.shape, F32)

    locals_[0].wait()

    def turn(source, half):
        @pl.loop(0, 8)
        def _(k):
            rows = pl.ds(pl.multiple_of(k * BLOCK, BLOCK), BLOCK)
            lanes = pl.ds(pl.multiple_of(half * ROWS, ROWS), ROWS)
            high, low = halves(source[:, rows].T)
            ht_hi[rows, lanes] = high
            ht_lo[rows, lanes] = low

    turn(h_own, core)
    to_h.wait()
    turn(h_sib, 1 - core)
    locals_[1].wait()
    locals_[3].wait()
    past.from_sibling(0, 0, 0)
    block_product(0, chip)

    for batch in past.stage1():
        for copy in batch:
            copy.start()
    for i in range(1, 4):
        past.from_sibling(i, *SIB[i])
        block_product(0, near(*SIB[i]))
    for batch in past.stage2():
        for copy in batch:
            copy.start()

    @pl.when(lag != 0)
    def _():
        remote(e_view, e_view, in_send.at[1], in_recv.at[1], next_group).wait_recv()
        for copy in older.start():
            copy.start()

    for i in range(4, 7):
        past.from_sibling(i, *SIB[i])
        block_product(0, near(*SIB[i]))
    for batch in past.stage3():
        for copy in batch:
            copy.start()
    locals_[2].wait()
    past.from_sibling(7, *SIB[7])
    block_product(0, near(*SIB[7]))

    @pl.when(lag != 0)
    def _():
        for batch in older.stage1():
            for copy in batch:
                copy.start()

    owner = lax.broadcasted_iota(jnp.int32, (EXC, ROWS), 0) % 64 // 8
    my_half = pl.ds(pl.multiple_of(core * 64, 64), 64)
    other_half = pl.ds(pl.multiple_of((1 - core) * 64, 64), 64)
    my_lanes = pl.ds(pl.multiple_of(core * ROWS, ROWS), ROWS)
    other_lanes = pl.ds(pl.multiple_of((1 - core) * ROWS, ROWS), ROWS)

    def c_copy(n):
        return remote(ct.at[n, other_half], hb.at[n, :, my_lanes], c_send.at[n], c_recv.at[n], sibling)

    def c_arrived(n):
        view = hb.at[n, :, other_lanes]
        remote(view, view, c_send.at[n], c_recv.at[n], sibling).wait_recv()

    def finish_history(n):
        total = (acc[n, :, 0:EXC] + acc[n, :, EXC:]).T
        ct[n] = total - jnp.where(owner == lag, xv[n].T, 0.0)
        c_copy(n).start()
        hb[n, :, my_lanes] = ct[n, my_half]

    def r_start(n):
        for k in range(1, 8):
            other = lag_near(k)
            remote(ub.at[n, other], rb.at[n, k - 1], r_send.at[n], r_recv.at[n], at_lag(other)).start()

    def r_sum(n):
        view = rb.at[n]
        remote(view, view, r_send.at[n], r_recv.at[n], sibling).wait_recv()
        total = ub[n, lag]
        for k in range(7):
            total = total + rb[n, k]
        ab[n, chip] = -total

    def a_start(n):
        for dx, dz in NEAR[1:]:
            k = dx * 4 + dz - 1
            remote(
                ab.at[n, chip], ab.at[n, chip], a_send.at[n], a_recv.at[n, k], at_chip(near(dx, dz))
            ).start()

    def inverse(n):
        total = jnp.zeros((16, BLOCK), F32)
        for dx, dz in NEAR:
            source = near((2 - dx) % 2, (4 - dz) % 4)
            k = dx * 4 + dz - 1
            if k >= 0:
                view = ab.at[n, source]
                remote(view, view, a_send.at[n], a_recv.at[n, k], sibling).wait_recv()
            value = jnp.concatenate(halves(ab[n, source]), axis=0)
            rows = chip_rows(source)
            total = total + jnp.dot(value, ht_hi[rows, :], preferred_element_type=F32)
            total = total + jnp.dot(value, ht_lo[rows, :], preferred_element_type=F32)
        db[n] = total[0:8] + total[8:16]

    def m_copy(n, k):
        other = (chip + k) % 8
        return remote(db.at[n], mb.at[n, lag], m_send.at[n], m_recv.at[n], (chip, other * 2 + core))

    def m_start(n):
        @pl.when(lag != chip)
        def _():
            m_copy(n, 0).start()

        @pl.when(lag == chip)
        def _():
            mb[n, lag] = db[n]

        for k in range(1, 8):
            m_copy(n, k).start()

    def m_wait(n):
        def some(count):
            view = mb.at[n, pl.ds(0, count)]
            copy = remote(view, view, m_send.at[n], m_recv.at[n], sibling)
            copy.wait()

        @pl.when(lag != chip)
        def _():
            some(8)

        @pl.when(lag == chip)
        def _():
            some(7)

    def o_start(n):
        ob[n, lag] = db[n]
        for k in range(1, 8):
            remote(db.at[n], ob.at[n, lag], o_send.at[n], o_recv.at[n], at_lag(lag_near(k))).start()

    def o_sib(n):
        return remote(ob.at[n, :, :, other_lanes], sb.at[n], os_send.at[n], os_recv.at[n], sibling)

    def o_pass(n):
        view = ob.at[n, pl.ds(0, 7)]
        remote(view, view, o_send.at[n], o_recv.at[n], sibling).wait_recv()
        o_sib(n).start()

    def o_finish(n):
        o_sib(n).wait_recv()
        out_ref[n, my_half] = ob[n, :, :, my_lanes].reshape(64, ROWS)
        out_ref[n, other_half] = sb[n].reshape(64, ROWS)

    def products(n, of):
        value = jnp.concatenate(halves(mb[of].reshape(64, BLOCK)), axis=0)
        high, low = halves(w12[n])
        total = lax.dot_general(value, high, NT, preferred_element_type=F32)
        total = total + lax.dot_general(value, low, NT, preferred_element_type=F32)
        return total[0:64] + total[64:128]

    def history_blocks(n, first, last):
        @pl.loop(first, last)
        def _(k):
            block_product(n, k)

    finish_history(0)
    w_pass(0)

    @pl.when(lag != 0)
    def _():
        for batch in older.stage2():
            for copy in batch:
                copy.start()

    c_arrived(0)
    ub[0] = hb[0].reshape(8, 8, BLOCK)
    r_start(0)
    w_pass(1)
    r_sum(0)
    a_start(0)

    @pl.when(lag != 0)
    def _():
        for batch in older.stage3():
            for copy in batch:
                copy.start()
        for i in range(8):
            older.from_sibling(i, *SIB[i])

    inverse(0)
    m_start(0)
    o_start(0)
    history_blocks(1, 0, 8)
    finish_history(1)
    w_sib_arrived(0)
    w_sib_arrived(1)
    c_arrived(1)
    m_wait(0)
    ub[1] = (hb[1] + products(0, 0)).reshape(8, 8, BLOCK)
    r_start(1)
    history_blocks(2, 0, 4)
    r_sum(1)
    a_start(1)
    history_blocks(2, 4, 8)
    finish_history(2)
    inverse(1)
    m_start(1)
    o_start(1)
    c_arrived(2)
    later = hb[2] + products(1, 0)
    o_pass(0)
    m_wait(1)
    ub[2] = (later + products(0, 1)).reshape(8, 8, BLOCK)
    r_start(2)
    o_finish(0)
    o_pass(1)
    r_sum(2)
    a_start(2)
    o_finish(1)
    inverse(2)
    o_start(2)
    o_pass(2)

    for copy in past.everything():
        copy.wait_send()

    @pl.when(lag != 0)
    def _():
        for copy in older.everything():
            copy.wait_send()

    @pl.when(lag < 7)
    def _():
        handed.wait_send()

    @pl.when(lag == 0)
    def _():
        for n in range(2):
            view = w_hbm.at[n, :, pl.ds(0, 7 * BLOCK)]
            pltpu.make_async_copy(view, view, w_send.at[n]).wait()

    for n in range(2):
        w_sib(n).wait_send()
    for n in range(STEPS):
        c_copy(n).wait_send()
        view = rb.at[n]
        remote(view, view, r_send.at[n], r_recv.at[n], sibling).wait_send()
        view = ab.at[n, pl.ds(0, 7)]
        remote(view, view, a_send.at[n], a_recv.at[n, 0], sibling).wait_send()
        view = ob.at[n, pl.ds(0, 7)]
        remote(view, view, o_send.at[n], o_recv.at[n], sibling).wait_send()
        o_sib(n).wait_send()
    o_finish(2)


def on_device(lag_weights, inverse_head, excitation, history):
    vmem = pltpu.VMEM
    dma = pltpu.SemaphoreType.DMA
    turned = pl.pallas_call(
        kernel,
        out_shape=jax.ShapeDtypeStruct((STEPS, EXC, ROWS), F32),
        in_specs=[pl.BlockSpec(memory_space=pl.ANY)] * 4,
        out_specs=pl.BlockSpec(memory_space=pltpu.VMEM),
        scratch_shapes=[
            vmem((LAGS, ROWS, M), F32),
            vmem((LAGS + 2, M, EXC), F32),
            vmem((ROWS, M), F32),
            vmem((ROWS, M), F32),
            vmem((M, BLOCK), BF16),
            vmem((M, BLOCK), BF16),
            vmem((2, BLOCK, BLOCK), F32),
            vmem((STEPS, ROWS, EXC), F32),
            vmem((STEPS, ROWS, 2 * EXC), F32),
            vmem((STEPS, EXC, ROWS), F32),
            vmem((STEPS, 64, BLOCK), F32),
            vmem((STEPS, 8, 8, BLOCK), F32),
            vmem((STEPS, 7, 8, BLOCK), F32),
            vmem((STEPS, 8, 8, BLOCK), F32),
            vmem((STEPS, 8, BLOCK), F32),
            vmem((2, 8, 8, BLOCK), F32),
            vmem((STEPS, 8, 8, BLOCK), F32),
            vmem((STEPS, 8, 8, ROWS), F32),
            dma((6,)),
            dma((12,)), dma((12,)), dma((8,)), dma((8,)),
            dma((12,)), dma((12,)), dma((8,)), dma((8,)),
            dma((4,)), dma((4,)), dma((2,)), dma((2,)),
            dma((STEPS,)), dma((STEPS,)), dma((STEPS,)), dma((STEPS,)),
            dma((STEPS,)), dma((STEPS, 7)), dma((2,)), dma((2,)),
            dma((STEPS,)), dma((STEPS,)), dma((STEPS,)), dma((STEPS,)),
        ],
        compiler_params=pltpu.CompilerParams(
            collective_id=0, has_side_effects=True, vmem_limit_bytes=58 << 20
        ),
        name="steps",
    )(lag_weights, inverse_head, excitation, history)
    return jnp.swapaxes(turned, 1, 2)


def solution(mesh):
    placed = (P("lag", "row", None), P("row", None), P(None, "row", None), P("lag", "row", None))
    return jax.shard_map(
        on_device, mesh=mesh, in_specs=placed, out_specs=P(None, "row", None), check_vma=False
    )
```

```python
import jax
import jax.numpy as jnp
from jax import lax
from jax.experimental import pallas as pl
from jax.experimental.pallas import tpu as pltpu
from jax.sharding import PartitionSpec as P

STEPS = 3
LAGS = 4
ROWS = 256
M = 4096
EXC = 128
BLOCK = 512
F32 = jnp.float32
BF16 = jnp.bfloat16
MESH = pl.DeviceIdType.MESH
NT = (((1,), (1,)), ((), ()))
NEAR = ((0, 0), (0, 1), (0, 3), (1, 0), (0, 2), (1, 1), (1, 3), (1, 2))


def halves(value):
    high = value.astype(BF16)
    return high, (value - high.astype(F32)).astype(BF16)


def kernel(
    w_hbm, h_hbm, x_hbm, p_hbm, out_ref,
    wv, pg, h_own, h_sib, ht_hi, ht_lo, w12, xv, acc,
    ct, hb, ub, rb, r0, ab, db, mb,
    local_sem, p_send, p_recv, s_send, s_recv, n_send, n_recv, ns_send, ns_recv,
    e_send, e_recv, es_send, es_recv,
    w_send, w_recv, in_send, in_recv, c_send, c_recv, r_send, r_recv,
    a_send, a_recv, m_send, m_recv, o_send, o_recv,
):
    lag = lax.axis_index("lag")
    row = lax.axis_index("row")
    chip, core = row // 2, row % 2
    y, x_lo = lag // 2, lag % 2
    x_hi, z = chip // 4, chip % 4

    def near(dx, dz):
        return ((x_hi + dx) % 2) * 4 + (z + dz) % 4

    def at_chip(other):
        return (lag, other * 2 + core)

    def lag_near(k):
        return ((y + k // 2) % 4) * 2 + (x_lo + k % 2) % 2

    def at_lag(other):
        return (other, row)

    sibling = (lag, chip * 2 + 1 - core)

    def rows_of(a_chip, a_core):
        return pl.ds(pl.multiple_of((a_chip * 2 + a_core) * ROWS, ROWS), ROWS)

    def chip_rows(a_chip):
        return pl.ds(pl.multiple_of(a_chip * BLOCK, BLOCK), BLOCK)

    def remote(src, dst, send, recv, device):
        return pltpu.make_async_remote_copy(
            src_ref=src, dst_ref=dst, send_sem=send, recv_sem=recv,
            device_id=device, device_id_type=MESH,
        )

    def holder_of(a_chip):
        return (a_chip // 4) * (2 + 4 * ((a_chip // 2) % 2))

    holder = holder_of(chip)
    slot = (1 - chip // 4) * chip + (chip // 4) * (chip % 2)
    at_home = lag == holder
    HOLDERS = ((0, 0, 4), (2, 4, 2), (6, 6, 2))

    mine = rows_of(chip, core)
    locals_ = [
        pltpu.make_async_copy(h_hbm, h_own, local_sem.at[0]),
        pltpu.make_async_copy(p_hbm, pg.at[pl.ds(2, LAGS), mine], local_sem.at[1]),
        pltpu.make_async_copy(x_hbm, xv, local_sem.at[2]),
        pltpu.make_async_copy(w_hbm, wv, local_sem.at[3]),
    ]
    for copy in locals_:
        copy.start()

    barrier = pltpu.get_barrier_semaphore()

    def greet(device):
        pl.semaphore_signal(barrier, inc=1, device_id=device, device_id_type=MESH)

    greet(sibling)
    for k in range(1, 8):
        greet(at_chip(near(k // 4, k % 4)))
        greet(at_lag(lag_near(k)))
        greet((lag_near(k), chip * 2 + 1 - core))
    for who, first, count in HOLDERS:

        @pl.when(lag == who)
        def _():
            for source in range(first, first + count):
                for other in range(8):
                    if other == who:

                        @pl.when(chip != source)
                        def _():
                            greet((other, source * 2 + core))
                    else:
                        greet((other, source * 2 + core))

    @pl.when(at_home)
    def _():
        pl.semaphore_wait(barrier, 29)

    @pl.when(jnp.logical_not(at_home))
    def _():
        pl.semaphore_wait(barrier, 30)

    up, down, across = at_chip(near(0, 1)), at_chip(near(0, 3)), at_chip(near(1, 0))

    class Gather:
        def __init__(self, first, count, send, recv, ssend, srecv):
            self.first, self.count = first, count
            self.send, self.recv, self.ssend, self.srecv = send, recv, ssend, srecv
            self.all = (first, count, 0, ROWS)
            if count == LAGS:
                self.low, self.high = (first, 2, 0, ROWS), (first + 2, 2, 0, ROWS)
                self.b1, self.b2 = (first + 2, 1, 0, ROWS), (first + 3, 1, 0, ROWS)
            else:
                self.low, self.high = (first, 1, 0, 128), (first, 1, 128, 128)
                self.b1, self.b2 = (first, 1, 128, 64), (first, 1, 192, 64)

        def view(self, dx, dz, part, a_core=None):
            start, count, offset, size = part
            base = (near(dx, dz) * 2 + (core if a_core is None else a_core)) * ROWS + offset
            return pg.at[pl.ds(start, count), pl.ds(pl.multiple_of(base, 64), size)]

        def copy(self, index, dx, dz, part, device, src=None):
            view = self.view(dx, dz, part)
            return remote(view if src is None else src, view, self.send.at[index], self.recv.at[index], device)

        def arrived(self, index, dx, dz, part):
            view = self.view(dx, dz, part)
            remote(view, view, self.send.at[index], self.recv.at[index], up).wait_recv()

        def to_sibling(self, dx, dz, src=None):
            index = dx * 4 + dz
            view = self.view(dx, dz, self.all)
            return remote(view if src is None else src, view, self.ssend.at[index], self.srecv.at[index], sibling)

        def from_sibling(self, index):
            view = self.view(index // 4, index % 4, self.all, 1 - core)
            remote(view, view, self.ssend.at[index], self.srecv.at[index], sibling).wait_recv()

        def start(self, src=None):
            return [
                self.copy(0, 0, 0, self.all, up, src),
                self.copy(1, 0, 0, self.all, down, src),
                self.copy(2, 0, 0, self.all, across, src),
                self.to_sibling(0, 0, src),
            ]

        def stage1(self):
            self.arrived(0, 0, 3, self.all)
            out = [self.copy(3, 0, 3, self.low, up), self.copy(5, 0, 3, self.low, across), self.to_sibling(0, 3)]
            yield out
            self.arrived(1, 0, 1, self.all)
            out = [self.copy(4, 0, 1, self.high, down), self.copy(6, 0, 1, self.low, across), self.to_sibling(0, 1)]
            yield out
            self.arrived(2, 1, 0, self.all)
            yield [self.copy(8, 1, 0, self.high, up), self.copy(9, 1, 0, self.high, down), self.to_sibling(1, 0)]

        def stage2(self):
            self.arrived(3, 0, 2, self.low)
            yield [self.copy(7, 0, 2, self.low, across)]
            self.arrived(4, 0, 2, self.high)
            yield [self.to_sibling(0, 2)]
            self.arrived(8, 1, 3, self.high)
            yield [self.copy(10, 1, 3, self.b1, up)]
            self.arrived(9, 1, 1, self.high)
            yield [self.copy(11, 1, 1, self.b2, down)]
            self.arrived(5, 1, 3, self.low)
            yield [self.to_sibling(1, 3)]
            self.arrived(6, 1, 1, self.low)
            yield [self.to_sibling(1, 1)]

        def stage3(self):
            self.arrived(7, 1, 2, self.low)
            self.arrived(10, 1, 2, self.b1)
            self.arrived(11, 1, 2, self.b2)
            yield [self.to_sibling(1, 2)]

        def everything(self):
            return (
                [self.copy(i, 0, 0, self.all, up) for i in range(3)]
                + [self.copy(i, 0, 0, self.low, up) for i in range(3, 10)]
                + [self.copy(i, 0, 0, self.b1, up) for i in (10, 11)]
                + [self.to_sibling(i // 4, i % 4) for i in range(8)]
            )

    def place(i):
        close = 2 * i - i // 3 - (i + 7) // 8
        far = 3 * i - 10 - i // 6 - 4 * (i // 7)
        return (1 - i // 4) * close + (i // 4) * far

    past = Gather(2, LAGS, p_send, p_recv, s_send, s_recv)
    newer = Gather(1, 1, n_send, n_recv, ns_send, ns_recv)
    older = Gather(0, 1, e_send, e_recv, es_send, es_recv)

    for copy in past.start(p_hbm):
        copy.start()
    to_h = remote(h_hbm, h_sib, in_send.at[0], in_recv.at[0], sibling)
    to_h.start()

    e_view = pg.at[pl.ds(0, 2), mine]
    next_group = ((lag + 1) % 8, row)
    handed = remote(p_hbm.at[pl.ds(2, 2)], e_view, in_send.at[1], in_recv.at[1], next_group)

    def w_half(n, half):
        return w12.at[n, :, pl.ds(pl.multiple_of(half * 2 * BLOCK, 2 * BLOCK), 2 * BLOCK)]

    def w_from(n, first, count):
        return w_hbm.at[n, :, pl.ds(first * BLOCK, count * BLOCK)]

    def w_copy(n, who, first, count):
        return remote(w_from(n, first, count), w_half(n, core), w_send.at[n], w_recv.at[n], (who, row))

    def w_sib(n, who):
        src, dst = (w_from(n, 0, 4), w12.at[n]) if who == 0 else (w_half(n, core), w_half(n, core))
        return remote(src, dst, w_send.at[2 + n], w_recv.at[2 + n], sibling)

    def w_start(n):
        @pl.when(lag == 0)
        def _():
            for held in HOLDERS[1:]:
                w_copy(n, *held).start()
            w_sib(n, 0).start()

    def w_pass(n):
        for who, first, count in HOLDERS[1:]:

            @pl.when(lag == who)
            def _():
                w_copy(n, who, first, count).wait_recv()
                w_sib(n, who).start()

    def w_wait(n):
        for who, _, _ in HOLDERS:

            @pl.when(lag == who)
            def _():
                w_sib(n, who).wait_recv()

    w_start(0)
    w_start(1)

    @pl.when(lag < 7)
    def _():
        handed.start()

    @pl.when(lag == 0)
    def _():
        pg[0:2] = jnp.zeros((2, M, EXC), F32)

    def block_product(n, a_chip, first=0, last=LAGS):
        rows = chip_rows(a_chip)
        values, highs, lows = [], [], []
        for i in range(first, last):
            values.append(jnp.concatenate(halves(pg[2 + i - n, rows, :]), axis=1))
            high, low = halves(wv[i, :, rows])
            highs.append(high)
            lows.append(low)
        value = jnp.concatenate(values, axis=0)
        acc[n] += jnp.dot(jnp.concatenate(highs, axis=1), value, preferred_element_type=F32) + jnp.dot(
            jnp.concatenate(lows, axis=1), value, preferred_element_type=F32
        )

    acc[...] = jnp.zeros(acc.shape, F32)

    locals_[0].wait()

    def turn(source, half):
        @pl.loop(0, 8)
        def _(k):
            rows = pl.ds(pl.multiple_of(k * BLOCK, BLOCK), BLOCK)
            lanes = pl.ds(pl.multiple_of(half * ROWS, ROWS), ROWS)
            high, low = halves(source[:, rows].T)
            ht_hi[rows, lanes] = high
            ht_lo[rows, lanes] = low

    turn(h_own, core)
    to_h.wait()
    turn(h_sib, 1 - core)
    locals_[1].wait()
    locals_[3].wait()

    def run(copies):
        for batch in copies:
            for copy in batch:
                copy.start()

    def outer(copies):
        @pl.when(lag != 0)
        def _():
            run(copies())

    locals_[2].wait()

    @pl.loop(0, 8)
    def _(i):
        @pl.when(i == 1)
        def _():
            run(past.stage1())

        @pl.when(i == 4)
        def _():
            run(past.stage2())

            @pl.when(lag != 0)
            def _():
                remote(e_view, e_view, in_send.at[1], in_recv.at[1], next_group).wait_recv()
                run([newer.start()])

        @pl.when(i == 7)
        def _():
            run(past.stage3())
            outer(newer.stage1)

        k = place(i)
        past.from_sibling(k)
        block_product(0, near(k // 4, k % 4))

    owner = lax.broadcasted_iota(jnp.int32, (EXC, ROWS), 0) % 64 // 8
    my_half = pl.ds(pl.multiple_of(core * 64, 64), 64)
    other_half = pl.ds(pl.multiple_of((1 - core) * 64, 64), 64)
    my_lanes = pl.ds(pl.multiple_of(core * ROWS, ROWS), ROWS)
    other_lanes = pl.ds(pl.multiple_of((1 - core) * ROWS, ROWS), ROWS)

    def c_copy(n):
        return remote(ct.at[n, other_half], hb.at[n, :, my_lanes], c_send.at[n], c_recv.at[n], sibling)

    def c_arrived(n):
        view = hb.at[n, :, other_lanes]
        remote(view, view, c_send.at[n], c_recv.at[n], sibling).wait_recv()

    def turn_history(n):
        total = (acc[n, :, 0:EXC] + acc[n, :, EXC:]).T
        ct[n] = total - jnp.where(owner == lag, xv[n].T, 0.0)

    def finish_history(n):
        turn_history(n)
        c_copy(n).start()
        hb[n, :, my_lanes] = ct[n, my_half]

    def eight(a_core, a_lag):
        return pl.ds(pl.multiple_of(a_core * 64 + a_lag * 8, 8), 8)

    def r_first():
        for k in range(8):
            for other_core in (1 - core, core) if k else (1 - core,):
                other = lag_near(k)
                remote(
                    ct.at[0, eight(other_core, other)], r0.at[k, :, my_lanes],
                    r_send.at[0], r_recv.at[0 if k else STEPS], (other, chip * 2 + other_core),
                ).start()
        r0[0, :, my_lanes] = ct[0, eight(core, lag)]

    def r_first_sum():
        view = r0.at[pl.ds(1, 7)]
        remote(view, view, r_send.at[0], r_recv.at[0], sibling).wait_recv()
        view = r0.at[0, :, other_lanes]
        remote(view, view, r_send.at[0], r_recv.at[STEPS], sibling).wait_recv()
        total = r0[0]
        for k in range(1, 8):
            total = total + r0[k]
        ab[0, chip] = -total

    def r_start(n):
        for k in range(1, 8):
            other = lag_near(k)
            remote(ub.at[n, other], rb.at[n, k - 1], r_send.at[n], r_recv.at[n], at_lag(other)).start()

    def r_sum(n):
        view = rb.at[n]
        remote(view, view, r_send.at[n], r_recv.at[n], sibling).wait_recv()
        total = ub[n, lag]
        for k in range(7):
            total = total + rb[n, k]
        ab[n, chip] = -total

    def a_start(n):
        for dx, dz in NEAR[1:]:
            k = dx * 4 + dz
            remote(
                ab.at[n, chip], ab.at[n, chip], a_send.at[n], a_recv.at[n, k], at_chip(near(dx, dz))
            ).start()

    def inverse(n):
        def pair(j, total):
            for i in (2 * j, 2 * j + 1):
                k = place(i)
                source = near(2 - k // 4, 4 - k % 4)

                @pl.when(k > 0)
                def _():
                    view = ab.at[n, source]
                    remote(view, view, a_send.at[n], a_recv.at[n, k], sibling).wait_recv()

                value = jnp.concatenate(halves(ab[n, source]), axis=0)
                rows = chip_rows(source)
                total = total + jnp.dot(value, ht_hi[rows, :], preferred_element_type=F32)
                total = total + jnp.dot(value, ht_lo[rows, :], preferred_element_type=F32)
            return total

        total = lax.fori_loop(0, 4, pair, jnp.zeros((16, BLOCK), F32))
        db[n] = total[0:8] + total[8:16]

    def m_copy(n, k):
        other = (chip + k) % 8
        return remote(db.at[n], mb.at[n, slot * 8 + lag], m_send.at[n], m_recv.at[n], (holder, other * 2 + core))

    def m_start(n):
        for k in range(1, 8):
            m_copy(n, k).start()

        @pl.when(jnp.logical_not(at_home))
        def _():
            m_copy(n, 0).start()

        @pl.when(at_home)
        def _():
            mb[n, slot * 8 + lag] = db[n]

    def m_wait(n):
        def some(count):
            view = mb.at[n, pl.ds(0, count)]
            remote(view, view, m_send.at[n], m_recv.at[n], sibling).wait_recv()

        for who, _, count in HOLDERS:

            @pl.when(jnp.logical_and(lag == who, at_home))
            def _():
                some(count * 8 - 1)

            @pl.when(jnp.logical_and(lag == who, jnp.logical_not(at_home)))
            def _():
                some(count * 8)

    def m_sent(n):
        def some(count):
            view = mb.at[n, pl.ds(0, count)]
            remote(view, view, m_send.at[n], m_recv.at[n], sibling).wait_send()

        @pl.when(at_home)
        def _():
            some(7)

        @pl.when(jnp.logical_not(at_home))
        def _():
            some(8)

    def o_start(n):
        spot = eight(core, lag)
        for k in range(8):
            for other_core in (1 - core, core) if k else (1 - core,):
                lanes = pl.ds(pl.multiple_of(other_core * ROWS, ROWS), ROWS)
                remote(
                    db.at[n, :, lanes], out_ref.at[n, spot],
                    o_send.at[n], o_recv.at[n], (lag_near(k), chip * 2 + other_core),
                ).start()
        out_ref[n, spot] = db[n, :, my_lanes]

    def o_done(n):
        view = out_ref.at[n, pl.ds(0, 120)]
        remote(view, view, o_send.at[n], o_recv.at[n], sibling).wait()

    def add_products(n, of):
        def add(ref, start, part, lanes):
            values = mb[of, pl.ds(part * 8, 8)].reshape(64, BLOCK)
            value = jnp.concatenate(halves(values), axis=0)
            high, low = halves(ref[n, :, pl.ds(pl.multiple_of(start, BLOCK), BLOCK)])
            total = lax.dot_general(value, high, NT, preferred_element_type=F32)
            total = total + lax.dot_general(value, low, NT, preferred_element_type=F32)
            hb[n + of + 1, :, lanes] += total[0:64] + total[64:128]

        @pl.when(lag == 0)
        def _():
            @pl.loop(0, 4)
            def _(part):
                add(wv, part * BLOCK, part, my_lanes)
                add(w12, part * BLOCK, part, other_lanes)

        @pl.when(jnp.logical_or(lag == 2, lag == 6))
        def _():
            @pl.loop(0, 2)
            def _(part):
                add(w12, (core * 2 + part) * BLOCK, part, my_lanes)
                add(w12, (2 - core * 2 + part) * BLOCK, part, other_lanes)

    def history_blocks(n, first, last, lags):
        @pl.loop(first, last)
        def _(k):
            block_product(n, k, *lags)

    def whole(gather):
        @pl.when(lag != 0)
        def _():
            for i in range(8):
                gather.from_sibling(i)

    turn_history(0)
    r_first()
    history_blocks(1, 0, 4, (1, 4))
    r_first_sum()
    a_start(0)
    outer(newer.stage2)
    history_blocks(1, 4, 8, (1, 4))
    w_pass(0)
    inverse(0)
    m_start(0)
    o_start(0)
    outer(newer.stage3)
    outer(lambda: [older.start()])
    history_blocks(2, 0, 8, (2, 4))
    whole(newer)
    history_blocks(1, 0, 8, (0, 1))
    finish_history(1)
    w_wait(0)
    outer(older.stage1)
    m_wait(0)
    c_arrived(1)
    add_products(0, 0)
    ub[1] = hb[1].reshape(8, 8, BLOCK)
    r_start(1)
    w_pass(1)
    r_sum(1)
    a_start(1)
    outer(older.stage2)
    inverse(1)
    m_start(1)
    o_start(1)
    outer(older.stage3)
    whole(older)
    history_blocks(2, 0, 8, (0, 2))
    finish_history(2)
    c_arrived(2)
    w_wait(1)
    add_products(1, 0)
    m_wait(1)
    add_products(0, 1)
    ub[2] = hb[2].reshape(8, 8, BLOCK)
    r_start(2)
    o_done(0)
    r_sum(2)
    a_start(2)
    o_done(1)
    inverse(2)
    o_start(2)

    for copy in past.everything():
        copy.wait_send()

    @pl.when(lag != 0)
    def _():
        for copy in newer.everything() + older.everything():
            copy.wait_send()

    @pl.when(lag < 7)
    def _():
        handed.wait_send()

    for n in range(2):
        m_sent(n)

        @pl.when(lag == 0)
        def _():
            view = w_from(n, 4, 4)
            pltpu.make_async_copy(view, view, w_send.at[n]).wait()

        for who, _, _ in HOLDERS:

            @pl.when(lag == who)
            def _():
                w_sib(n, who).wait_send()

    view = ct.at[0, pl.ds(0, 120)]
    remote(view, view, r_send.at[0], r_recv.at[0], sibling).wait_send()
    for n in range(STEPS):
        if n > 0:
            c_copy(n).wait_send()
            view = rb.at[n]
            remote(view, view, r_send.at[n], r_recv.at[n], sibling).wait_send()
        view = ab.at[n, pl.ds(0, 7)]
        remote(view, view, a_send.at[n], a_recv.at[n, 1], sibling).wait_send()
    o_done(2)


def on_device(lag_weights, inverse_head, excitation, history):
    vmem = pltpu.VMEM
    dma = pltpu.SemaphoreType.DMA
    turned = pl.pallas_call(
        kernel,
        out_shape=jax.ShapeDtypeStruct((STEPS, EXC, ROWS), F32),
        in_specs=[pl.BlockSpec(memory_space=pl.ANY)] * 4,
        out_specs=pl.BlockSpec(memory_space=pltpu.VMEM),
        scratch_shapes=[
            vmem((LAGS, ROWS, M), F32),
            vmem((LAGS + 2, M, EXC), F32),
            vmem((ROWS, M), F32),
            vmem((ROWS, M), F32),
            vmem((M, BLOCK), BF16),
            vmem((M, BLOCK), BF16),
            vmem((2, ROWS, 4 * BLOCK), F32),
            vmem((STEPS, ROWS, EXC), F32),
            vmem((STEPS, ROWS, 2 * EXC), F32),
            vmem((STEPS, EXC, ROWS), F32),
            vmem((STEPS, 64, BLOCK), F32),
            vmem((STEPS, 8, 8, BLOCK), F32),
            vmem((STEPS, 7, 8, BLOCK), F32),
            vmem((8, 8, BLOCK), F32),
            vmem((STEPS, 8, 8, BLOCK), F32),
            vmem((STEPS, 8, BLOCK), F32),
            vmem((2, 32, 8, BLOCK), F32),
            dma((6,)),
            dma((12,)), dma((12,)), dma((8,)), dma((8,)),
            dma((12,)), dma((12,)), dma((8,)), dma((8,)),
            dma((12,)), dma((12,)), dma((8,)), dma((8,)),
            dma((4,)), dma((4,)), dma((2,)), dma((2,)),
            dma((STEPS,)), dma((STEPS,)), dma((STEPS,)), dma((STEPS + 1,)),
            dma((STEPS,)), dma((STEPS, 8)), dma((2,)), dma((2,)),
            dma((STEPS,)), dma((STEPS,)),
        ],
        compiler_params=pltpu.CompilerParams(
            collective_id=0, has_side_effects=True, vmem_limit_bytes=58 << 20
        ),
        name="steps",
    )(lag_weights, inverse_head, excitation, history)
    return jnp.swapaxes(turned, 1, 2)


def solution(mesh):
    placed = (P("lag", "row", None), P("row", None), P(None, "row", None), P("lag", "row", None))
    return jax.shard_map(
        on_device, mesh=mesh, in_specs=placed, out_specs=P(None, "row", None), check_vma=False
    )
```

```python
import jax
import jax.numpy as jnp
from jax import lax
from jax.experimental import pallas as pl
from jax.experimental.pallas import tpu as pltpu
from jax.sharding import PartitionSpec as P

STEPS = 3
LAGS = 4
ROWS = 256
M = 4096
EXC = 128
BLOCK = 512
F32 = jnp.float32
BF16 = jnp.bfloat16
MESH = pl.DeviceIdType.MESH
NT = (((1,), (1,)), ((), ()))
NEAR = ((0, 0), (0, 1), (0, 3), (1, 0), (0, 2), (1, 1), (1, 3), (1, 2))


def halves(value):
    high = value.astype(BF16)
    return high, (value - high.astype(F32)).astype(BF16)


def kernel(
    w_hbm, h_hbm, x_hbm, p_hbm, out_ref,
    wv, pg, h_own, h_sib, ht_hi, ht_lo, w12, xv, acc,
    ct, hb, ub, rb, r0, ab, db, mb,
    local_sem, p_send, p_recv, s_send, s_recv, n_send, n_recv, ns_send, ns_recv,
    e_send, e_recv, es_send, es_recv,
    w_send, w_recv, in_send, in_recv, c_send, c_recv, r_send, r_recv,
    a_send, a_recv, m_send, m_recv, o_send, o_recv,
):
    lag = lax.axis_index("lag")
    row = lax.axis_index("row")
    chip, core = row // 2, row % 2
    y, x_lo = lag // 2, lag % 2
    x_hi, z = chip // 4, chip % 4

    def near(dx, dz):
        return ((x_hi + dx) % 2) * 4 + (z + dz) % 4

    def at_chip(other):
        return (lag, other * 2 + core)

    def lag_near(k):
        return ((y + k // 2) % 4) * 2 + (x_lo + k % 2) % 2

    def at_lag(other):
        return (other, row)

    sibling = (lag, chip * 2 + 1 - core)

    def rows_of(a_chip, a_core):
        return pl.ds(pl.multiple_of((a_chip * 2 + a_core) * ROWS, ROWS), ROWS)

    def chip_rows(a_chip):
        return pl.ds(pl.multiple_of(a_chip * BLOCK, BLOCK), BLOCK)

    def remote(src, dst, send, recv, device):
        return pltpu.make_async_remote_copy(
            src_ref=src, dst_ref=dst, send_sem=send, recv_sem=recv,
            device_id=device, device_id_type=MESH,
        )

    def holder_of(a_chip):
        return (a_chip // 4) * (2 + 4 * ((a_chip // 2) % 2))

    holder = holder_of(chip)
    slot = (1 - chip // 4) * chip + (chip // 4) * (chip % 2)
    at_home = lag == holder
    HOLDERS = ((0, 0, 4), (2, 4, 2), (6, 6, 2))

    mine = rows_of(chip, core)
    locals_ = [
        pltpu.make_async_copy(h_hbm, h_own, local_sem.at[0]),
        pltpu.make_async_copy(p_hbm, pg.at[pl.ds(2, LAGS), mine], local_sem.at[1]),
        pltpu.make_async_copy(x_hbm, xv, local_sem.at[2]),
        pltpu.make_async_copy(w_hbm, wv, local_sem.at[3]),
    ]
    for copy in locals_:
        copy.start()

    barrier = pltpu.get_barrier_semaphore()

    def greet(device):
        pl.semaphore_signal(barrier, inc=1, device_id=device, device_id_type=MESH)

    greet(sibling)
    for k in range(1, 8):
        greet(at_chip(near(k // 4, k % 4)))
        greet(at_lag(lag_near(k)))
        greet((lag_near(k), chip * 2 + 1 - core))
    for who, first, count in HOLDERS:

        @pl.when(lag == who)
        def _():
            for source in range(first, first + count):
                for other in range(8):
                    if other == who:

                        @pl.when(chip != source)
                        def _():
                            greet((other, source * 2 + core))
                    else:
                        greet((other, source * 2 + core))

    @pl.when(at_home)
    def _():
        pl.semaphore_wait(barrier, 29)

    @pl.when(jnp.logical_not(at_home))
    def _():
        pl.semaphore_wait(barrier, 30)

    up, down, across = at_chip(near(0, 1)), at_chip(near(0, 3)), at_chip(near(1, 0))

    class Gather:
        def __init__(self, first, count, send, recv, ssend, srecv):
            self.first, self.count = first, count
            self.send, self.recv, self.ssend, self.srecv = send, recv, ssend, srecv
            self.all = (first, count, 0, ROWS)
            if count == LAGS:
                self.low, self.high = (first, 2, 0, ROWS), (first + 2, 2, 0, ROWS)
                self.b1, self.b2 = (first + 2, 1, 0, ROWS), (first + 3, 1, 0, ROWS)
            else:
                self.low, self.high = (first, 1, 0, 128), (first, 1, 128, 128)
                self.b1, self.b2 = (first, 1, 128, 64), (first, 1, 192, 64)

        def view(self, dx, dz, part, a_core=None):
            start, count, offset, size = part
            base = (near(dx, dz) * 2 + (core if a_core is None else a_core)) * ROWS + offset
            return pg.at[pl.ds(start, count), pl.ds(pl.multiple_of(base, 64), size)]

        def copy(self, index, dx, dz, part, device, src=None):
            view = self.view(dx, dz, part)
            return remote(view if src is None else src, view, self.send.at[index], self.recv.at[index], device)

        def arrived(self, index, dx, dz, part):
            view = self.view(dx, dz, part)
            remote(view, view, self.send.at[index], self.recv.at[index], up).wait_recv()

        def to_sibling(self, dx, dz, src=None):
            index = dx * 4 + dz
            view = self.view(dx, dz, self.all)
            return remote(view if src is None else src, view, self.ssend.at[index], self.srecv.at[index], sibling)

        def from_sibling(self, index):
            view = self.view(index // 4, index % 4, self.all, 1 - core)
            remote(view, view, self.ssend.at[index], self.srecv.at[index], sibling).wait_recv()

        def start(self, src=None):
            return [
                self.copy(0, 0, 0, self.all, up, src),
                self.copy(1, 0, 0, self.all, down, src),
                self.copy(2, 0, 0, self.all, across, src),
                self.to_sibling(0, 0, src),
            ]

        def stage1(self):
            self.arrived(0, 0, 3, self.all)
            out = [self.copy(3, 0, 3, self.low, up), self.copy(5, 0, 3, self.low, across), self.to_sibling(0, 3)]
            yield out
            self.arrived(1, 0, 1, self.all)
            out = [self.copy(4, 0, 1, self.high, down), self.copy(6, 0, 1, self.low, across), self.to_sibling(0, 1)]
            yield out
            self.arrived(2, 1, 0, self.all)
            yield [self.copy(8, 1, 0, self.high, up), self.copy(9, 1, 0, self.high, down), self.to_sibling(1, 0)]

        def stage2(self):
            self.arrived(3, 0, 2, self.low)
            yield [self.copy(7, 0, 2, self.low, across)]
            self.arrived(4, 0, 2, self.high)
            yield [self.to_sibling(0, 2)]
            self.arrived(8, 1, 3, self.high)
            yield [self.copy(10, 1, 3, self.b1, up)]
            self.arrived(9, 1, 1, self.high)
            yield [self.copy(11, 1, 1, self.b2, down)]
            self.arrived(5, 1, 3, self.low)
            yield [self.to_sibling(1, 3)]
            self.arrived(6, 1, 1, self.low)
            yield [self.to_sibling(1, 1)]

        def stage3(self):
            self.arrived(7, 1, 2, self.low)
            self.arrived(10, 1, 2, self.b1)
            self.arrived(11, 1, 2, self.b2)
            yield [self.to_sibling(1, 2)]

        def everything(self):
            return (
                [self.copy(i, 0, 0, self.all, up) for i in range(3)]
                + [self.copy(i, 0, 0, self.low, up) for i in range(3, 10)]
                + [self.copy(i, 0, 0, self.b1, up) for i in (10, 11)]
                + [self.to_sibling(i // 4, i % 4) for i in range(8)]
            )

    def place(i):
        close = 2 * i - i // 3 - (i + 7) // 8
        far = 3 * i - 10 - i // 6 - 4 * (i // 7)
        return (1 - i // 4) * close + (i // 4) * far

    past = Gather(2, LAGS, p_send, p_recv, s_send, s_recv)
    newer = Gather(1, 1, n_send, n_recv, ns_send, ns_recv)
    older = Gather(0, 1, e_send, e_recv, es_send, es_recv)
    fresh = Gather(LAGS + 2, 1, n_send, n_recv, ns_send, ns_recv)
    before = 1 + 5 * (lag == 0).astype(jnp.int32)

    for copy in past.start(p_hbm):
        copy.start()
    to_h = remote(h_hbm, h_sib, in_send.at[0], in_recv.at[0], sibling)
    to_h.start()

    e_view = pg.at[pl.ds(0, 2), mine]
    next_group = ((lag + 1) % 8, row)
    handed = remote(p_hbm.at[pl.ds(2, 2)], e_view, in_send.at[1], in_recv.at[1], next_group)

    def w_half(n, half):
        return w12.at[n, :, pl.ds(pl.multiple_of(half * 2 * BLOCK, 2 * BLOCK), 2 * BLOCK)]

    def w_from(n, first, count):
        return w_hbm.at[n, :, pl.ds(first * BLOCK, count * BLOCK)]

    def w_copy(n, who, first, count):
        return remote(w_from(n, first, count), w_half(n, core), w_send.at[n], w_recv.at[n], (who, row))

    def w_sib(n, who):
        src, dst = (w_from(n, 0, 4), w12.at[n]) if who == 0 else (w_half(n, core), w_half(n, core))
        return remote(src, dst, w_send.at[2 + n], w_recv.at[2 + n], sibling)

    def w_start(n):
        @pl.when(lag == 0)
        def _():
            for held in HOLDERS[1:]:
                w_copy(n, *held).start()
            w_sib(n, 0).start()

    def w_pass(n):
        for who, first, count in HOLDERS[1:]:

            @pl.when(lag == who)
            def _():
                w_copy(n, who, first, count).wait_recv()
                w_sib(n, who).start()

    def w_wait(n):
        for who, _, _ in HOLDERS:

            @pl.when(lag == who)
            def _():
                w_sib(n, who).wait_recv()

    w_start(0)

    @pl.when(lag < 7)
    def _():
        handed.start()

    @pl.when(lag == 0)
    def _():
        pg[0:2] = jnp.zeros((2, M, EXC), F32)

    def block_product(n, a_chip, first=0, last=LAGS):
        rows = chip_rows(a_chip)
        values, highs, lows = [], [], []
        for i in range(first, last):
            slot = before if (n, i) == (2, 1) else 2 + i - n
            values.append(jnp.concatenate(halves(pg[slot, rows, :]), axis=1))
            high, low = halves(wv[i, :, rows])
            highs.append(high)
            lows.append(low)
        value = jnp.concatenate(values, axis=0)
        acc[n] += jnp.dot(jnp.concatenate(highs, axis=1), value, preferred_element_type=F32) + jnp.dot(
            jnp.concatenate(lows, axis=1), value, preferred_element_type=F32
        )

    acc[...] = jnp.zeros(acc.shape, F32)

    locals_[0].wait()

    def turn(source, half):
        @pl.loop(0, 8)
        def _(k):
            rows = pl.ds(pl.multiple_of(k * BLOCK, BLOCK), BLOCK)
            lanes = pl.ds(pl.multiple_of(half * ROWS, ROWS), ROWS)
            high, low = halves(source[:, rows].T)
            ht_hi[rows, lanes] = high
            ht_lo[rows, lanes] = low

    turn(h_own, core)
    to_h.wait()
    turn(h_sib, 1 - core)
    locals_[1].wait()
    locals_[3].wait()

    def run(copies):
        for batch in copies:
            for copy in batch:
                copy.start()

    def outer(copies):
        @pl.when(lag != 0)
        def _():
            run(copies())

    locals_[2].wait()

    @pl.loop(0, 8)
    def _(i):
        @pl.when(i == 1)
        def _():
            run(past.stage1())

        @pl.when(i == 4)
        def _():
            run(past.stage2())

            @pl.when(lag != 0)
            def _():
                remote(e_view, e_view, in_send.at[1], in_recv.at[1], next_group).wait_recv()
                run([newer.start()])

        @pl.when(i == 7)
        def _():
            run(past.stage3())
            outer(newer.stage1)

        k = place(i)
        past.from_sibling(k)
        block_product(0, near(k // 4, k % 4))

    owner = lax.broadcasted_iota(jnp.int32, (EXC, ROWS), 0) % 64 // 8
    my_half = pl.ds(pl.multiple_of(core * 64, 64), 64)
    other_half = pl.ds(pl.multiple_of((1 - core) * 64, 64), 64)
    my_lanes = pl.ds(pl.multiple_of(core * ROWS, ROWS), ROWS)
    other_lanes = pl.ds(pl.multiple_of((1 - core) * ROWS, ROWS), ROWS)

    def c_copy(n):
        return remote(ct.at[n, other_half], hb.at[n, :, my_lanes], c_send.at[n], c_recv.at[n], sibling)

    def c_arrived(n):
        view = hb.at[n, :, other_lanes]
        remote(view, view, c_send.at[n], c_recv.at[n], sibling).wait_recv()

    def turn_history(n):
        total = (acc[n, :, 0:EXC] + acc[n, :, EXC:]).T
        ct[n] = total - jnp.where(owner == lag, xv[n].T, 0.0)

    def finish_history(n):
        turn_history(n)
        c_copy(n).start()
        hb[n, :, my_lanes] = ct[n, my_half]

    def eight(a_core, a_lag):
        return pl.ds(pl.multiple_of(a_core * 64 + a_lag * 8, 8), 8)

    def r_first():
        for k in range(8):
            for other_core in (1 - core, core) if k else (1 - core,):
                other = lag_near(k)
                remote(
                    ct.at[0, eight(other_core, other)], r0.at[k, :, my_lanes],
                    r_send.at[0], r_recv.at[0 if k else STEPS], (other, chip * 2 + other_core),
                ).start()
        r0[0, :, my_lanes] = ct[0, eight(core, lag)]

    def r_first_sum():
        view = r0.at[pl.ds(1, 7)]
        remote(view, view, r_send.at[0], r_recv.at[0], sibling).wait_recv()
        view = r0.at[0, :, other_lanes]
        remote(view, view, r_send.at[0], r_recv.at[STEPS], sibling).wait_recv()
        total = r0[0]
        for k in range(1, 8):
            total = total + r0[k]
        ab[0, chip] = -total

    def r_start(n):
        for k in range(1, 8):
            other = lag_near(k)
            remote(ub.at[n, other], rb.at[n, k - 1], r_send.at[n], r_recv.at[n], at_lag(other)).start()

    def r_sum(n):
        view = rb.at[n]
        remote(view, view, r_send.at[n], r_recv.at[n], sibling).wait_recv()
        total = ub[n, lag]
        for k in range(7):
            total = total + rb[n, k]
        ab[n, chip] = -total

    def a_start(n):
        for dx, dz in NEAR[1:]:
            k = dx * 4 + dz
            remote(
                ab.at[n, chip], ab.at[n, chip], a_send.at[n], a_recv.at[n, k], at_chip(near(dx, dz))
            ).start()

    def inverse(n):
        def pair(j, total):
            for i in (2 * j, 2 * j + 1):
                k = place(i)
                source = near(2 - k // 4, 4 - k % 4)

                @pl.when(k > 0)
                def _():
                    view = ab.at[n, source]
                    remote(view, view, a_send.at[n], a_recv.at[n, k], sibling).wait_recv()

                value = jnp.concatenate(halves(ab[n, source]), axis=0)
                rows = chip_rows(source)
                total = total + jnp.dot(value, ht_hi[rows, :], preferred_element_type=F32)
                total = total + jnp.dot(value, ht_lo[rows, :], preferred_element_type=F32)
            return total

        total = lax.fori_loop(0, 4, pair, jnp.zeros((16, BLOCK), F32))
        db[n] = total[0:8] + total[8:16]

    def m_copy(n, k):
        other = (chip + k) % 8
        return remote(db.at[n], mb.at[n, slot * 8 + lag], m_send.at[n], m_recv.at[n], (holder, other * 2 + core))

    def m_start(n):
        for k in range(1, 8):
            m_copy(n, k).start()

        @pl.when(jnp.logical_not(at_home))
        def _():
            m_copy(n, 0).start()

        @pl.when(at_home)
        def _():
            mb[n, slot * 8 + lag] = db[n]

    def m_wait(n):
        def some(count):
            view = mb.at[n, pl.ds(0, count)]
            remote(view, view, m_send.at[n], m_recv.at[n], sibling).wait_recv()

        for who, _, count in HOLDERS:

            @pl.when(jnp.logical_and(lag == who, at_home))
            def _():
                some(count * 8 - 1)

            @pl.when(jnp.logical_and(lag == who, jnp.logical_not(at_home)))
            def _():
                some(count * 8)

    def m_sent(n):
        def some(count):
            view = mb.at[n, pl.ds(0, count)]
            remote(view, view, m_send.at[n], m_recv.at[n], sibling).wait_send()

        @pl.when(at_home)
        def _():
            some(7)

        @pl.when(jnp.logical_not(at_home))
        def _():
            some(8)

    def o_start(n):
        spot = eight(core, lag)
        for k in range(8):
            for other_core in (1 - core, core) if k else (1 - core,):
                lanes = pl.ds(pl.multiple_of(other_core * ROWS, ROWS), ROWS)
                remote(
                    db.at[n, :, lanes], out_ref.at[n, spot],
                    o_send.at[n], o_recv.at[n], (lag_near(k), chip * 2 + other_core),
                ).start()
        out_ref[n, spot] = db[n, :, my_lanes]

    def o_done(n):
        view = out_ref.at[n, pl.ds(0, 120)]
        remote(view, view, o_send.at[n], o_recv.at[n], sibling).wait()

    def add_products(n, of):
        def add(ref, start, part, lanes):
            values = mb[of, pl.ds(part * 8, 8)].reshape(64, BLOCK)
            value = jnp.concatenate(halves(values), axis=0)
            high, low = halves(ref[n, :, pl.ds(pl.multiple_of(start, BLOCK), BLOCK)])
            total = lax.dot_general(value, high, NT, preferred_element_type=F32)
            total = total + lax.dot_general(value, low, NT, preferred_element_type=F32)
            hb[n + of + 1, :, lanes] += total[0:64] + total[64:128]

        @pl.when(lag == 0)
        def _():
            @pl.loop(0, 4)
            def _(part):
                add(wv, part * BLOCK, part, my_lanes)
                add(w12, part * BLOCK, part, other_lanes)

        @pl.when(jnp.logical_or(lag == 2, lag == 6))
        def _():
            @pl.loop(0, 2)
            def _(part):
                add(w12, (core * 2 + part) * BLOCK, part, my_lanes)
                add(w12, (2 - core * 2 + part) * BLOCK, part, other_lanes)

    def history_blocks(n, first, last, lags):
        @pl.loop(first, last)
        def _(k):
            block_product(n, k, *lags)

    def whole(gather):
        @pl.when(lag != 0)
        def _():
            for i in range(8):
                gather.from_sibling(i)

    turn_history(0)
    r_first()
    history_blocks(1, 0, 4, (1, 4))
    r_first_sum()
    a_start(0)
    outer(newer.stage2)
    history_blocks(1, 4, 8, (1, 4))
    w_pass(0)
    inverse(0)
    m_start(0)
    o_start(0)
    outer(newer.stage3)
    outer(lambda: [older.start()])
    history_blocks(2, 0, 8, (2, 4))
    whole(newer)
    history_blocks(1, 0, 8, (0, 1))
    finish_history(1)
    outer(older.stage1)
    o_done(0)

    def first_only(copies):
        @pl.when(lag == 0)
        def _():
            run(copies())

    @pl.when(lag == 0)
    def _():
        pg[LAGS + 2, mine] = out_ref[0].T
        run([fresh.start()])

    w_wait(0)
    m_wait(0)
    c_arrived(1)
    add_products(0, 0)
    ub[1] = hb[1].reshape(8, 8, BLOCK)
    r_start(1)
    first_only(fresh.stage1)
    r_sum(1)
    a_start(1)
    outer(older.stage2)
    first_only(fresh.stage2)
    inverse(1)
    m_start(1)
    o_start(1)
    outer(older.stage3)
    whole(older)

    @pl.when(lag == 0)
    def _():
        run(fresh.stage3())
        for i in range(8):
            fresh.from_sibling(i)

    history_blocks(2, 0, 8, (0, 2))
    finish_history(2)
    c_arrived(2)
    m_wait(1)
    add_products(0, 1)
    ub[2] = hb[2].reshape(8, 8, BLOCK)
    r_start(2)
    r_sum(2)
    a_start(2)
    o_done(1)
    inverse(2)
    o_start(2)

    for copy in past.everything():
        copy.wait_send()

    for copy in newer.everything():
        copy.wait_send()

    @pl.when(lag != 0)
    def _():
        for copy in older.everything():
            copy.wait_send()

    @pl.when(lag < 7)
    def _():
        handed.wait_send()

    for n in range(2):
        m_sent(n)

    @pl.when(lag == 0)
    def _():
        view = w_from(0, 4, 4)
        pltpu.make_async_copy(view, view, w_send.at[0]).wait()

    for who, _, _ in HOLDERS:

        @pl.when(lag == who)
        def _():
            w_sib(0, who).wait_send()

    view = ct.at[0, pl.ds(0, 120)]
    remote(view, view, r_send.at[0], r_recv.at[0], sibling).wait_send()
    for n in range(STEPS):
        if n > 0:
            c_copy(n).wait_send()
            view = rb.at[n]
            remote(view, view, r_send.at[n], r_recv.at[n], sibling).wait_send()
        view = ab.at[n, pl.ds(0, 7)]
        remote(view, view, a_send.at[n], a_recv.at[n, 1], sibling).wait_send()
    o_done(2)


def on_device(lag_weights, inverse_head, excitation, history):
    vmem = pltpu.VMEM
    dma = pltpu.SemaphoreType.DMA
    turned = pl.pallas_call(
        kernel,
        out_shape=jax.ShapeDtypeStruct((STEPS, EXC, ROWS), F32),
        in_specs=[pl.BlockSpec(memory_space=pl.ANY)] * 4,
        out_specs=pl.BlockSpec(memory_space=pltpu.VMEM),
        scratch_shapes=[
            vmem((LAGS, ROWS, M), F32),
            vmem((LAGS + 3, M, EXC), F32),
            vmem((ROWS, M), F32),
            vmem((ROWS, M), F32),
            vmem((M, BLOCK), BF16),
            vmem((M, BLOCK), BF16),
            vmem((1, ROWS, 4 * BLOCK), F32),
            vmem((STEPS, ROWS, EXC), F32),
            vmem((STEPS, ROWS, 2 * EXC), F32),
            vmem((STEPS, EXC, ROWS), F32),
            vmem((STEPS, 64, BLOCK), F32),
            vmem((STEPS, 8, 8, BLOCK), F32),
            vmem((STEPS, 7, 8, BLOCK), F32),
            vmem((8, 8, BLOCK), F32),
            vmem((STEPS, 8, 8, BLOCK), F32),
            vmem((STEPS, 8, BLOCK), F32),
            vmem((2, 32, 8, BLOCK), F32),
            dma((6,)),
            dma((12,)), dma((12,)), dma((8,)), dma((8,)),
            dma((12,)), dma((12,)), dma((8,)), dma((8,)),
            dma((12,)), dma((12,)), dma((8,)), dma((8,)),
            dma((4,)), dma((4,)), dma((2,)), dma((2,)),
            dma((STEPS,)), dma((STEPS,)), dma((STEPS,)), dma((STEPS + 1,)),
            dma((STEPS,)), dma((STEPS, 8)), dma((2,)), dma((2,)),
            dma((STEPS,)), dma((STEPS,)),
        ],
        compiler_params=pltpu.CompilerParams(
            collective_id=0, has_side_effects=True, vmem_limit_bytes=58 << 20
        ),
        name="steps",
    )(lag_weights, inverse_head, excitation, history)
    return jnp.swapaxes(turned, 1, 2)


def solution(mesh):
    placed = (P("lag", "row", None), P("row", None), P(None, "row", None), P("lag", "row", None))
    return jax.shard_map(
        on_device, mesh=mesh, in_specs=placed, out_specs=P(None, "row", None), check_vma=False
    )
```

```python
import jax
import jax.numpy as jnp
from jax import lax
from jax.experimental import pallas as pl
from jax.experimental.pallas import tpu as pltpu
from jax.sharding import PartitionSpec as P

STEPS = 3
LAGS = 4
ROWS = 256
M = 4096
EXC = 128
BLOCK = 512
F32 = jnp.float32
BF16 = jnp.bfloat16
MESH = pl.DeviceIdType.MESH
NT = (((1,), (1,)), ((), ()))
NEAR = ((0, 0), (0, 1), (0, 3), (1, 0), (0, 2), (1, 1), (1, 3), (1, 2))


def halves(value):
    high = value.astype(BF16)
    return high, (value - high.astype(F32)).astype(BF16)


def kernel(
    w_hbm, h_hbm, x_hbm, p_hbm, out_ref,
    wv, pg, h_own, h_sib, ht_hi, ht_lo, w12, xv, acc,
    ct, hb, ub, rb, r0, ab, db, mb,
    local_sem, p_send, p_recv, s_send, s_recv, n_send, n_recv, ns_send, ns_recv,
    e_send, e_recv, es_send, es_recv,
    w_send, w_recv, in_send, in_recv, c_send, c_recv, r_send, r_recv,
    a_send, a_recv, m_send, m_recv, o_send, o_recv,
):
    lag = lax.axis_index("lag")
    row = lax.axis_index("row")
    chip, core = row // 2, row % 2
    y, x_lo = lag // 2, lag % 2
    x_hi, z = chip // 4, chip % 4

    def near(dx, dz):
        return ((x_hi + dx) % 2) * 4 + (z + dz) % 4

    def at_chip(other):
        return (lag, other * 2 + core)

    def lag_near(k):
        return ((y + k // 2) % 4) * 2 + (x_lo + k % 2) % 2

    def at_lag(other):
        return (other, row)

    sibling = (lag, chip * 2 + 1 - core)

    def rows_of(a_chip, a_core):
        return pl.ds(pl.multiple_of((a_chip * 2 + a_core) * ROWS, ROWS), ROWS)

    def chip_rows(a_chip):
        return pl.ds(pl.multiple_of(a_chip * BLOCK, BLOCK), BLOCK)

    def remote(src, dst, send, recv, device):
        return pltpu.make_async_remote_copy(
            src_ref=src, dst_ref=dst, send_sem=send, recv_sem=recv,
            device_id=device, device_id_type=MESH,
        )

    def holder_of(a_chip):
        return (a_chip // 4) * (2 + 4 * ((a_chip // 2) % 2))

    holder = holder_of(chip)
    slot = (1 - chip // 4) * chip + (chip // 4) * (chip % 2)
    at_home = lag == holder
    HOLDERS = ((0, 0, 4), (2, 4, 2), (6, 6, 2))

    mine = rows_of(chip, core)
    locals_ = [
        pltpu.make_async_copy(h_hbm, h_own, local_sem.at[0]),
        pltpu.make_async_copy(p_hbm, pg.at[pl.ds(2, LAGS), mine], local_sem.at[1]),
        pltpu.make_async_copy(x_hbm, xv, local_sem.at[2]),
        pltpu.make_async_copy(w_hbm, wv, local_sem.at[3]),
    ]
    for copy in locals_:
        copy.start()

    barrier = pltpu.get_barrier_semaphore()

    def greet(device):
        pl.semaphore_signal(barrier, inc=1, device_id=device, device_id_type=MESH)

    greet(sibling)
    for k in range(1, 8):
        greet(at_chip(near(k // 4, k % 4)))
        greet(at_lag(lag_near(k)))
        greet((lag_near(k), chip * 2 + 1 - core))
    for who, first, count in HOLDERS:

        @pl.when(lag == who)
        def _():
            for source in range(first, first + count):
                for other in range(8):
                    if other == who:

                        @pl.when(chip != source)
                        def _():
                            greet((other, source * 2 + core))
                    else:
                        greet((other, source * 2 + core))

    @pl.when(at_home)
    def _():
        pl.semaphore_wait(barrier, 29)

    @pl.when(jnp.logical_not(at_home))
    def _():
        pl.semaphore_wait(barrier, 30)

    up, down, across = at_chip(near(0, 1)), at_chip(near(0, 3)), at_chip(near(1, 0))

    class Gather:
        def __init__(self, first, count, send, recv, ssend, srecv):
            self.first, self.count = first, count
            self.send, self.recv, self.ssend, self.srecv = send, recv, ssend, srecv
            self.all = (first, count, 0, ROWS)
            if count == LAGS:
                self.low, self.high = (first, 2, 0, ROWS), (first + 2, 2, 0, ROWS)
                self.b1, self.b2 = (first + 2, 1, 0, ROWS), (first + 3, 1, 0, ROWS)
            else:
                self.low, self.high = (first, 1, 0, 128), (first, 1, 128, 128)
                self.b1, self.b2 = (first, 1, 128, 64), (first, 1, 192, 64)

        def view(self, dx, dz, part, a_core=None):
            start, count, offset, size = part
            base = (near(dx, dz) * 2 + (core if a_core is None else a_core)) * ROWS + offset
            return pg.at[pl.ds(start, count), pl.ds(pl.multiple_of(base, 64), size)]

        def copy(self, index, dx, dz, part, device, src=None):
            view = self.view(dx, dz, part)
            return remote(view if src is None else src, view, self.send.at[index], self.recv.at[index], device)

        def arrived(self, index, dx, dz, part):
            view = self.view(dx, dz, part)
            remote(view, view, self.send.at[index], self.recv.at[index], up).wait_recv()

        def to_sibling(self, dx, dz, src=None):
            index = dx * 4 + dz
            view = self.view(dx, dz, self.all)
            return remote(view if src is None else src, view, self.ssend.at[index], self.srecv.at[index], sibling)

        def from_sibling(self, index):
            view = self.view(index // 4, index % 4, self.all, 1 - core)
            remote(view, view, self.ssend.at[index], self.srecv.at[index], sibling).wait_recv()

        def start(self, src=None):
            return [
                self.copy(0, 0, 0, self.all, up, src),
                self.copy(1, 0, 0, self.all, down, src),
                self.copy(2, 0, 0, self.all, across, src),
                self.to_sibling(0, 0, src),
            ]

        def stage1(self):
            self.arrived(0, 0, 3, self.all)
            out = [self.copy(3, 0, 3, self.low, up), self.copy(5, 0, 3, self.low, across), self.to_sibling(0, 3)]
            yield out
            self.arrived(1, 0, 1, self.all)
            out = [self.copy(4, 0, 1, self.high, down), self.copy(6, 0, 1, self.low, across), self.to_sibling(0, 1)]
            yield out
            self.arrived(2, 1, 0, self.all)
            yield [self.copy(8, 1, 0, self.high, up), self.copy(9, 1, 0, self.high, down), self.to_sibling(1, 0)]

        def stage2(self):
            self.arrived(3, 0, 2, self.low)
            yield [self.copy(7, 0, 2, self.low, across)]
            self.arrived(4, 0, 2, self.high)
            yield [self.to_sibling(0, 2)]
            self.arrived(8, 1, 3, self.high)
            yield [self.copy(10, 1, 3, self.b1, up)]
            self.arrived(9, 1, 1, self.high)
            yield [self.copy(11, 1, 1, self.b2, down)]
            self.arrived(5, 1, 3, self.low)
            yield [self.to_sibling(1, 3)]
            self.arrived(6, 1, 1, self.low)
            yield [self.to_sibling(1, 1)]

        def stage3(self):
            self.arrived(7, 1, 2, self.low)
            self.arrived(10, 1, 2, self.b1)
            self.arrived(11, 1, 2, self.b2)
            yield [self.to_sibling(1, 2)]

        def everything(self):
            return (
                [self.copy(i, 0, 0, self.all, up) for i in range(3)]
                + [self.copy(i, 0, 0, self.low, up) for i in range(3, 10)]
                + [self.copy(i, 0, 0, self.b1, up) for i in (10, 11)]
                + [self.to_sibling(i // 4, i % 4) for i in range(8)]
            )

    def place(i):
        close = 2 * i - i // 3 - (i + 7) // 8
        far = 3 * i - 10 - i // 6 - 4 * (i // 7)
        return (1 - i // 4) * close + (i // 4) * far

    past = Gather(2, LAGS, p_send, p_recv, s_send, s_recv)
    newer = Gather(1, 1, n_send, n_recv, ns_send, ns_recv)
    older = Gather(0, 1, e_send, e_recv, es_send, es_recv)
    fresh = Gather(LAGS + 2, 1, n_send, n_recv, ns_send, ns_recv)
    before = 1 + 5 * (lag == 0).astype(jnp.int32)

    for copy in past.start(p_hbm):
        copy.start()
    to_h = remote(h_hbm, h_sib, in_send.at[0], in_recv.at[0], sibling)
    to_h.start()

    e_view = pg.at[pl.ds(0, 2), mine]
    next_group = ((lag + 1) % 8, row)
    handed = remote(p_hbm.at[pl.ds(2, 2)], e_view, in_send.at[1], in_recv.at[1], next_group)

    def w_half(n, half):
        return w12.at[n, :, pl.ds(pl.multiple_of(half * 2 * BLOCK, 2 * BLOCK), 2 * BLOCK)]

    def w_from(n, first, count):
        return w_hbm.at[n, :, pl.ds(first * BLOCK, count * BLOCK)]

    def w_copy(n, who, first, count):
        return remote(w_from(n, first, count), w_half(n, core), w_send.at[n], w_recv.at[n], (who, row))

    def w_sib(n, who):
        src, dst = (w_from(n, 0, 4), w12.at[n]) if who == 0 else (w_half(n, core), w_half(n, core))
        return remote(src, dst, w_send.at[2 + n], w_recv.at[2 + n], sibling)

    def w_start(n):
        @pl.when(lag == 0)
        def _():
            for held in HOLDERS[1:]:
                w_copy(n, *held).start()
            w_sib(n, 0).start()

    def w_pass(n):
        for who, first, count in HOLDERS[1:]:

            @pl.when(lag == who)
            def _():
                w_copy(n, who, first, count).wait_recv()
                w_sib(n, who).start()

    def w_wait(n):
        for who, _, _ in HOLDERS:

            @pl.when(lag == who)
            def _():
                w_sib(n, who).wait_recv()

    w_start(0)

    @pl.when(lag < 7)
    def _():
        handed.start()

    @pl.when(lag == 0)
    def _():
        pg[0:2] = jnp.zeros((2, M, EXC), F32)

    def block_product(n, a_chip, first=0, last=LAGS):
        rows = chip_rows(a_chip)
        values, highs, lows = [], [], []
        for i in range(first, last):
            slot = before if (n, i) == (2, 1) else 2 + i - n
            values.append(jnp.concatenate(halves(pg[slot, rows, :]), axis=1))
            high, low = halves(wv[i, :, rows])
            highs.append(high)
            lows.append(low)
        value = jnp.concatenate(values, axis=0)
        acc[n] += jnp.dot(jnp.concatenate(highs, axis=1), value, preferred_element_type=F32) + jnp.dot(
            jnp.concatenate(lows, axis=1), value, preferred_element_type=F32
        )

    acc[...] = jnp.zeros(acc.shape, F32)

    locals_[0].wait()

    def turn(source, half):
        @pl.loop(0, 8)
        def _(k):
            rows = pl.ds(pl.multiple_of(k * BLOCK, BLOCK), BLOCK)
            lanes = pl.ds(pl.multiple_of(half * ROWS, ROWS), ROWS)
            high, low = halves(source[:, rows].T)
            ht_hi[rows, lanes] = high
            ht_lo[rows, lanes] = low

    turn(h_own, core)
    to_h.wait()
    turn(h_sib, 1 - core)
    locals_[1].wait()
    locals_[3].wait()

    def run(copies):
        for batch in copies:
            for copy in batch:
                copy.start()

    def outer(copies):
        @pl.when(lag != 0)
        def _():
            run(copies())

    locals_[2].wait()

    @pl.loop(0, 8)
    def _(i):
        @pl.when(i == 1)
        def _():
            run(past.stage1())

        @pl.when(i == 4)
        def _():
            run(past.stage2())

            @pl.when(lag != 0)
            def _():
                remote(e_view, e_view, in_send.at[1], in_recv.at[1], next_group).wait_recv()
                run([newer.start()])

        @pl.when(i == 7)
        def _():
            run(past.stage3())
            outer(newer.stage1)

        k = place(i)
        past.from_sibling(k)
        block_product(0, near(k // 4, k % 4))

    owner = lax.broadcasted_iota(jnp.int32, (EXC, ROWS), 0) % 64 // 8
    my_half = pl.ds(pl.multiple_of(core * 64, 64), 64)
    other_half = pl.ds(pl.multiple_of((1 - core) * 64, 64), 64)
    my_lanes = pl.ds(pl.multiple_of(core * ROWS, ROWS), ROWS)
    other_lanes = pl.ds(pl.multiple_of((1 - core) * ROWS, ROWS), ROWS)

    def c_copy(n):
        return remote(ct.at[n, other_half], hb.at[n, :, my_lanes], c_send.at[n], c_recv.at[n], sibling)

    def c_arrived(n):
        view = hb.at[n, :, other_lanes]
        remote(view, view, c_send.at[n], c_recv.at[n], sibling).wait_recv()

    def turn_history(n):
        total = (acc[n, :, 0:EXC] + acc[n, :, EXC:]).T
        ct[n] = total - jnp.where(owner == lag, xv[n].T, 0.0)

    def finish_history(n):
        turn_history(n)
        c_copy(n).start()
        hb[n, :, my_lanes] = ct[n, my_half]

    def eight(a_core, a_lag):
        return pl.ds(pl.multiple_of(a_core * 64 + a_lag * 8, 8), 8)

    def r_first():
        for k in range(8):
            for other_core in (1 - core, core) if k else (1 - core,):
                other = lag_near(k)
                remote(
                    ct.at[0, eight(other_core, other)], r0.at[k, :, my_lanes],
                    r_send.at[0], r_recv.at[0 if k else STEPS], (other, chip * 2 + other_core),
                ).start()
        r0[0, :, my_lanes] = ct[0, eight(core, lag)]

    def r_first_sum():
        view = r0.at[pl.ds(1, 7)]
        remote(view, view, r_send.at[0], r_recv.at[0], sibling).wait_recv()
        view = r0.at[0, :, other_lanes]
        remote(view, view, r_send.at[0], r_recv.at[STEPS], sibling).wait_recv()
        total = r0[0]
        for k in range(1, 8):
            total = total + r0[k]
        ab[0, chip] = -total

    def r_start(n):
        for k in range(1, 8):
            other = lag_near(k)
            remote(ub.at[n, other], rb.at[n, k - 1], r_send.at[n], r_recv.at[n], at_lag(other)).start()

    def r_sum(n):
        view = rb.at[n]
        remote(view, view, r_send.at[n], r_recv.at[n], sibling).wait_recv()
        total = ub[n, lag]
        for k in range(7):
            total = total + rb[n, k]
        ab[n, chip] = -total

    def a_start(n):
        for dx, dz in NEAR[1:]:
            k = dx * 4 + dz
            remote(
                ab.at[n, chip], ab.at[n, chip], a_send.at[n], a_recv.at[n, k], at_chip(near(dx, dz))
            ).start()

    def inverse(n):
        total = jnp.zeros((16, BLOCK), F32)
        for i in range(8):
            k = place(i)
            source = near(2 - k // 4, 4 - k % 4)
            if k > 0:
                view = ab.at[n, source]
                remote(view, view, a_send.at[n], a_recv.at[n, k], sibling).wait_recv()
            value = jnp.concatenate(halves(ab[n, source]), axis=0)
            rows = chip_rows(source)
            total = total + jnp.dot(value, ht_hi[rows, :], preferred_element_type=F32)
            total = total + jnp.dot(value, ht_lo[rows, :], preferred_element_type=F32)
        db[n] = total[0:8] + total[8:16]

    def m_copy(n, k):
        other = (chip + k) % 8
        return remote(db.at[n], mb.at[n, slot * 8 + lag], m_send.at[n], m_recv.at[n], (holder, other * 2 + core))

    def m_start(n):
        for k in range(1, 8):
            m_copy(n, k).start()

        @pl.when(jnp.logical_not(at_home))
        def _():
            m_copy(n, 0).start()

        @pl.when(at_home)
        def _():
            mb[n, slot * 8 + lag] = db[n]

    def m_wait(n):
        def some(count):
            view = mb.at[n, pl.ds(0, count)]
            remote(view, view, m_send.at[n], m_recv.at[n], sibling).wait_recv()

        for who, _, count in HOLDERS:

            @pl.when(jnp.logical_and(lag == who, at_home))
            def _():
                some(count * 8 - 1)

            @pl.when(jnp.logical_and(lag == who, jnp.logical_not(at_home)))
            def _():
                some(count * 8)

    def m_sent(n):
        def some(count):
            view = mb.at[n, pl.ds(0, count)]
            remote(view, view, m_send.at[n], m_recv.at[n], sibling).wait_send()

        @pl.when(at_home)
        def _():
            some(7)

        @pl.when(jnp.logical_not(at_home))
        def _():
            some(8)

    def o_start(n):
        spot = eight(core, lag)
        for k in range(8):
            for other_core in (1 - core, core) if k else (1 - core,):
                lanes = pl.ds(pl.multiple_of(other_core * ROWS, ROWS), ROWS)
                remote(
                    db.at[n, :, lanes], out_ref.at[n, spot],
                    o_send.at[n], o_recv.at[n], (lag_near(k), chip * 2 + other_core),
                ).start()
        out_ref[n, spot] = db[n, :, my_lanes]

    def o_done(n):
        view = out_ref.at[n, pl.ds(0, 120)]
        remote(view, view, o_send.at[n], o_recv.at[n], sibling).wait()

    def add_products(n, of):
        def add(ref, start, part, lanes):
            values = mb[of, pl.ds(part * 8, 8)].reshape(64, BLOCK)
            value = jnp.concatenate(halves(values), axis=0)
            high, low = halves(ref[n, :, pl.ds(pl.multiple_of(start, BLOCK), BLOCK)])
            total = lax.dot_general(value, high, NT, preferred_element_type=F32)
            total = total + lax.dot_general(value, low, NT, preferred_element_type=F32)
            hb[n + of + 1, :, lanes] += total[0:64] + total[64:128]

        @pl.when(lag == 0)
        def _():
            @pl.loop(0, 4)
            def _(part):
                add(wv, part * BLOCK, part, my_lanes)
                add(w12, part * BLOCK, part, other_lanes)

        @pl.when(jnp.logical_or(lag == 2, lag == 6))
        def _():
            @pl.loop(0, 2)
            def _(part):
                add(w12, (core * 2 + part) * BLOCK, part, my_lanes)
                add(w12, (2 - core * 2 + part) * BLOCK, part, other_lanes)

    def history_blocks(n, first, last, lags):
        @pl.loop(first, last)
        def _(k):
            block_product(n, k, *lags)

    def whole(gather):
        @pl.when(lag != 0)
        def _():
            for i in range(8):
                gather.from_sibling(i)

    turn_history(0)
    r_first()
    history_blocks(1, 0, 4, (1, 4))
    r_first_sum()
    a_start(0)
    outer(newer.stage2)
    history_blocks(1, 4, 8, (1, 4))
    w_pass(0)
    inverse(0)
    m_start(0)
    o_start(0)
    outer(newer.stage3)
    outer(lambda: [older.start()])
    history_blocks(2, 0, 8, (2, 4))
    whole(newer)
    history_blocks(1, 0, 8, (0, 1))
    finish_history(1)
    outer(older.stage1)
    o_done(0)

    def first_only(copies):
        @pl.when(lag == 0)
        def _():
            run(copies())

    @pl.when(lag == 0)
    def _():
        pg[LAGS + 2, mine] = out_ref[0].T
        run([fresh.start()])

    w_wait(0)
    m_wait(0)
    c_arrived(1)
    add_products(0, 0)
    ub[1] = hb[1].reshape(8, 8, BLOCK)
    r_start(1)
    first_only(fresh.stage1)
    r_sum(1)
    a_start(1)
    outer(older.stage2)
    first_only(fresh.stage2)
    inverse(1)
    m_start(1)
    o_start(1)
    outer(older.stage3)
    whole(older)

    @pl.when(lag == 0)
    def _():
        run(fresh.stage3())
        for i in range(8):
            fresh.from_sibling(i)

    history_blocks(2, 0, 8, (0, 2))
    finish_history(2)
    c_arrived(2)
    m_wait(1)
    add_products(0, 1)
    ub[2] = hb[2].reshape(8, 8, BLOCK)
    r_start(2)
    r_sum(2)
    a_start(2)
    o_done(1)
    inverse(2)
    o_start(2)

    for copy in past.everything():
        copy.wait_send()

    for copy in newer.everything():
        copy.wait_send()

    @pl.when(lag != 0)
    def _():
        for copy in older.everything():
            copy.wait_send()

    @pl.when(lag < 7)
    def _():
        handed.wait_send()

    for n in range(2):
        m_sent(n)

    @pl.when(lag == 0)
    def _():
        view = w_from(0, 4, 4)
        pltpu.make_async_copy(view, view, w_send.at[0]).wait()

    for who, _, _ in HOLDERS:

        @pl.when(lag == who)
        def _():
            w_sib(0, who).wait_send()

    view = ct.at[0, pl.ds(0, 120)]
    remote(view, view, r_send.at[0], r_recv.at[0], sibling).wait_send()
    for n in range(STEPS):
        if n > 0:
            c_copy(n).wait_send()
            view = rb.at[n]
            remote(view, view, r_send.at[n], r_recv.at[n], sibling).wait_send()
        view = ab.at[n, pl.ds(0, 7)]
        remote(view, view, a_send.at[n], a_recv.at[n, 1], sibling).wait_send()
    o_done(2)


def on_device(lag_weights, inverse_head, excitation, history):
    vmem = pltpu.VMEM
    dma = pltpu.SemaphoreType.DMA
    turned = pl.pallas_call(
        kernel,
        out_shape=jax.ShapeDtypeStruct((STEPS, EXC, ROWS), F32),
        in_specs=[pl.BlockSpec(memory_space=pl.ANY)] * 4,
        out_specs=pl.BlockSpec(memory_space=pltpu.VMEM),
        scratch_shapes=[
            vmem((LAGS, ROWS, M), F32),
            vmem((LAGS + 3, M, EXC), F32),
            vmem((ROWS, M), F32),
            vmem((ROWS, M), F32),
            vmem((M, BLOCK), BF16),
            vmem((M, BLOCK), BF16),
            vmem((1, ROWS, 4 * BLOCK), F32),
            vmem((STEPS, ROWS, EXC), F32),
            vmem((STEPS, ROWS, 2 * EXC), F32),
            vmem((STEPS, EXC, ROWS), F32),
            vmem((STEPS, 64, BLOCK), F32),
            vmem((STEPS, 8, 8, BLOCK), F32),
            vmem((STEPS, 7, 8, BLOCK), F32),
            vmem((8, 8, BLOCK), F32),
            vmem((STEPS, 8, 8, BLOCK), F32),
            vmem((STEPS, 8, BLOCK), F32),
            vmem((2, 32, 8, BLOCK), F32),
            dma((6,)),
            dma((12,)), dma((12,)), dma((8,)), dma((8,)),
            dma((12,)), dma((12,)), dma((8,)), dma((8,)),
            dma((12,)), dma((12,)), dma((8,)), dma((8,)),
            dma((4,)), dma((4,)), dma((2,)), dma((2,)),
            dma((STEPS,)), dma((STEPS,)), dma((STEPS,)), dma((STEPS + 1,)),
            dma((STEPS,)), dma((STEPS, 8)), dma((2,)), dma((2,)),
            dma((STEPS,)), dma((STEPS,)),
        ],
        compiler_params=pltpu.CompilerParams(
            collective_id=0, has_side_effects=True, vmem_limit_bytes=58 << 20
        ),
        name="steps",
    )(lag_weights, inverse_head, excitation, history)
    return jnp.swapaxes(turned, 1, 2)


def solution(mesh):
    placed = (P("lag", "row", None), P("row", None), P(None, "row", None), P("lag", "row", None))
    return jax.shard_map(
        on_device, mesh=mesh, in_specs=placed, out_specs=P(None, "row", None), check_vma=False
    )
```
